256 devices in a mesh: seq: 64 (over z, y_hi, x), head: 4 (over y_lo, core).
Axes of the slice: x: 4, y: 4 (y_hi: 2, y_lo: 2; y = y_hi * 2 + y_lo), z: 8, core: 2. Of those that a mesh axis runs over, the one named last changes fastest.
Arguments:
- queries: bfloat16 [49152, 1536], P('seq', 'head'), may hold values from -24 to 24, as said below
- keys: bfloat16 [49152, 1536], P('seq', 'head'), may hold values from -24 to 24, as said below
- values: bfloat16 [49152, 1536], P('seq', 'head'), may hold values from -24 to 24
- learn_rate: float32 [4, 49152], P('head', 'seq'), may hold values from 0.02 to 0.5
- gate_fast: bfloat16 [4, 384, 384], P('head'), may hold values from -0.3125 to 0.3125
- up_fast: bfloat16 [4, 384, 384], P('head'), may hold values from -0.3125 to 0.3125
- down_fast: bfloat16 [4, 384, 384], P('head'), may hold values from -0.3125 to 0.3125
- ttt_gain: float32 [4, 384], P('head'), may hold values from 0.2 to 0.8
- out_weight: bfloat16 [1536, 1536], P('head'), may hold values from -0.15625 to 0.15625
Outputs:
- mixed: bfloat16 [49152, 1536], P('seq', 'head')
The draws below stay inside these ranges and needn't reach their ends.
Inputs may be any that keep to these rules, and one draw needn't show every extreme that they name: `queries`: real-valued activations. `keys`: real-valued activations.
All inputs are finite; a program needn't handle non-finite values.
Results may differ from the reference program's by a relative error of at most 0.014.
Values may be sent and summed in bfloat16 or wider, within the bound.
A program may use at most 128 MiB of HBM per device.

```python
import math
import jax
import jax.numpy as jnp
from jax import lax

D = 1536
HEADS = 4
FH = 384
TOK_DEV = 768
HD = 384
WINDOW = 3072
TOKENS = 49152


def paired_rows(key):
    query_key = jax.random.fold_in(key, 11)
    key_key = jax.random.fold_in(key, 12)
    query_base = jax.random.normal(query_key, (TOKENS, D), jnp.float32)
    key_base = jax.random.normal(key_key, (TOKENS, D), jnp.float32)
    key_new = key_base
    query_new = query_base
    return (jnp.clip(query_new, -24.0, 24.0), jnp.clip(key_new, -24.0, 24.0))


def draw_queries(key, part):
    return paired_rows(key)[0].astype(jnp.bfloat16)


def draw_keys(key, part):
    return paired_rows(key)[1].astype(jnp.bfloat16)


def block_levels(key, dims, cuts, least, high):
    level = 1.0
    for position, blocks in cuts:
        draws = jax.random.uniform(jax.random.fold_in(jax.random.fold_in(key, 6), position), (blocks,), jnp.float32, least / len(cuts), high / len(cuts))
        level = level * jnp.repeat(jnp.exp(draws), dims[position] // blocks).reshape((-1,) + (1,) * (len(dims) - 1 - position))
    return level


def bell_draw(key, dims, spread, most, split=(), kind=jnp.bfloat16):
    level = block_levels(key, dims, split, -0.22, 0.18) if split else 1.0
    values = jax.random.normal(key, dims, jnp.float32) * spread * level
    return jnp.minimum(jnp.maximum(values, -most), most).astype(kind)


def setup_inputs(seed: int = 0) -> dict:
    streams_of = jax.random.split(jax.random.key(seed), 10)
    return {
        "queries": draw_queries(jax.random.fold_in(streams_of[9], 71), 0),
        "keys": draw_keys(jax.random.fold_in(streams_of[9], 71), 0),
        "values": bell_draw(streams_of[2], (TOKENS, D), 4.0, 24.0, ((0, 64), (1, 4))),
        "learn_rate": jnp.clip(jnp.exp(math.log(0.5) - 3.218876 * jax.random.uniform(streams_of[3], (HEADS, TOKENS), jnp.float32) ** block_levels(streams_of[3], (HEADS, TOKENS), ((0, 4), (1, 64)), -0.2, 0.2)), 0.02, 0.5),
        "gate_fast": bell_draw(streams_of[4], (HEADS, HD, FH), HD ** -0.5, 0.3125, ((0, 4),)),
        "up_fast": bell_draw(streams_of[5], (HEADS, HD, FH), HD ** -0.5, 0.3125, ((0, 4),)),
        "down_fast": bell_draw(streams_of[6], (HEADS, FH, HD), FH ** -0.5, 0.3125, ((0, 4),)),
        "ttt_gain": jnp.clip(0.2 + 0.6 * jax.random.uniform(streams_of[7], (HEADS, HD), jnp.float32) ** block_levels(streams_of[7], (HEADS, HD), ((0, 4),), -0.2, 0.2), 0.2, 0.8),
        "out_weight": bell_draw(streams_of[8], (D, D), D ** -0.5, 0.15625, ((0, 4),)),
    }


ns_first = 3.4445
ns_second = -4.775
ns_third = 2.0315
big_negative = -1e+30

def pair_scores(left, right):
    return lax.dot_general(left, right, (((1,), (1,)), ((), ())), preferred_element_type=jnp.float32)

def token_sum(left, right):
    return lax.dot_general(left, right, (((0,), (0,)), ((), ())), preferred_element_type=jnp.float32)

def orthogonalize(grad):
    current = grad / (jnp.sqrt(jnp.sum(grad * grad)) + 1e-07)
    for sweep in range(5):
        square = jnp.dot(current, current.T, precision=lax.Precision.HIGHEST)
        mixer = ns_second * square + ns_third * jnp.dot(square, square, precision=lax.Precision.HIGHEST)
        current = ns_first * current + jnp.dot(mixer, current, precision=lax.Precision.HIGHEST)
    return current

def attend_head(query_head, key_head, value_head):
    head_size = query_head.shape[1]
    scale = head_size ** (-0.5)
    key_pad = jnp.concatenate([jnp.zeros((WINDOW, head_size), key_head.dtype), key_head], axis=0)
    value_pad = jnp.concatenate([jnp.zeros((WINDOW, head_size), value_head.dtype), value_head], axis=0)
    count = TOKENS // TOK_DEV

    def one_block(block):
        start = (block * TOK_DEV).astype(jnp.int32)
        query_rows = lax.dynamic_slice_in_dim(query_head, start, TOK_DEV, 0)
        key_rows = lax.dynamic_slice_in_dim(key_pad, start, WINDOW + TOK_DEV, 0)
        value_rows = lax.dynamic_slice_in_dim(value_pad, start, WINDOW + TOK_DEV, 0)
        scores = pair_scores(query_rows, key_rows) * scale
        query_pos = start + jnp.arange(TOK_DEV, dtype=jnp.int32)
        key_pos = start - WINDOW + jnp.arange(WINDOW + TOK_DEV, dtype=jnp.int32)
        valid = (key_pos[None, :] <= query_pos[:, None]) & (key_pos[None, :] > query_pos[:, None] - WINDOW) & (key_pos[None, :] >= 0)
        scores = jnp.where(valid, scores, big_negative)
        top = lax.optimization_barrier(jnp.max(scores, axis=1, keepdims=True))
        expo = jnp.where(valid, jnp.exp(scores - top), 0.0)
        total = lax.optimization_barrier(jnp.sum(expo, axis=1, keepdims=True))
        weighted = jnp.dot(expo.astype(jnp.bfloat16), value_rows, preferred_element_type=jnp.float32)
        return weighted / total
    blocks = lax.map(one_block, jnp.arange(count, dtype=jnp.int32))
    return blocks.reshape(TOKENS, head_size)

def fast_branch(query_head, key_head, value_head, rate, gate_w, up_w, down_w, gain):
    gate_k = jnp.dot(key_head, gate_w, preferred_element_type=jnp.float32)
    up_k = jnp.dot(key_head, up_w, preferred_element_type=jnp.float32)
    sig = jax.nn.sigmoid(gate_k)
    hidden_k = (gate_k * sig * up_k).astype(jnp.bfloat16)
    target = (-rate[:, None] * value_head.astype(jnp.float32)).astype(jnp.bfloat16)
    grad_down = token_sum(hidden_k, target)
    back = pair_scores(target, down_w)
    grad_gate_k = (back * up_k * sig * (1.0 + gate_k * (1.0 - sig))).astype(jnp.bfloat16)
    grad_up_k = (back * gate_k * sig).astype(jnp.bfloat16)
    grad_gate = token_sum(key_head, grad_gate_k)
    grad_up = token_sum(key_head, grad_up_k)
    gate_new = (gate_w.astype(jnp.float32) - orthogonalize(grad_gate)).astype(jnp.bfloat16)
    up_new = (up_w.astype(jnp.float32) - orthogonalize(grad_up)).astype(jnp.bfloat16)
    down_new = (down_w.astype(jnp.float32) - orthogonalize(grad_down)).astype(jnp.bfloat16)
    query_gate = jnp.dot(query_head, gate_new, preferred_element_type=jnp.float32)
    query_up = jnp.dot(query_head, up_new, preferred_element_type=jnp.float32)
    query_hidden = (query_gate * jax.nn.sigmoid(query_gate) * query_up).astype(jnp.bfloat16)
    fast_out = jnp.dot(query_hidden, down_new, preferred_element_type=jnp.float32)
    normed = fast_out * lax.rsqrt(lax.optimization_barrier(jnp.mean(fast_out * fast_out, axis=1, keepdims=True)) + 1e-06)
    return normed * gain[None, :]

def reference(queries, keys, values, learn_rate, gate_fast, up_fast, down_fast, ttt_gain, out_weight):
    head_size = D // HEADS
    pieces = []
    for head in range(HEADS):
        cols = slice(head * head_size, (head + 1) * head_size)
        query_head = queries[:, cols]
        key_head = keys[:, cols]
        value_head = values[:, cols]
        attended = attend_head(query_head, key_head, value_head)
        fast = fast_branch(query_head, key_head, value_head, learn_rate[head], gate_fast[head], up_fast[head], down_fast[head], ttt_gain[head])
        pieces.append((attended + fast).astype(jnp.bfloat16))
    combined = jnp.concatenate(pieces, axis=1)
    return jnp.dot(combined, out_weight, preferred_element_type=jnp.float32).astype(jnp.bfloat16)
```

```python
import functools

import jax
import jax.numpy as jnp
from jax import lax
from jax.experimental import pallas as pl
from jax.experimental.pallas import tpu as pltpu
from jax.sharding import Mesh
from jax.sharding import PartitionSpec as P

AXES = ("z", "yh", "x", "yl", "c")
SIZES = (8, 2, 4, 2, 2)
SEQ = ("z", "yh", "x")
HEAD = ("yl", "c")
BLOCKS = 64
PLANE = 16
MESH = pl.DeviceIdType.MESH
BF16 = jnp.bfloat16
F32 = jnp.float32

ns_first = 3.4445
ns_second = -4.775
ns_third = 2.0315
big_negative = -1e30
log2_e = 1.4426950408889634


def dot_nn(left, right):
    return lax.dot_general(left, right, (((1,), (0,)), ((), ())), preferred_element_type=F32)


def dot_nt(left, right):
    return lax.dot_general(left, right, (((1,), (1,)), ((), ())), preferred_element_type=F32)


def dot_tn(left, right):
    return lax.dot_general(left, right, (((0,), (0,)), ((), ())), preferred_element_type=F32)


def halves(wide):
    high = wide.astype(BF16)
    low = (wide - high.astype(F32)).astype(BF16)
    return high, low


def layer(
    q, k, v, lr, weights, gain, out_w,
    out,
    kh, vh, acc, top, total,
    hid, tgt, dgate, dup, part, psend, precv,
    zsend, zrecv, zsum, grad, left, right, stack, new,
    comb, wcol,
    row_s, row_r, d1_s, d1_r, d2_s, d2_r, d3_s, d3_r,
    xs_s, xs_r, zs_s, zs_r, ag_s, ag_r, bc_s, bc_r,
    w_s, w_r, hy_s, hy_r, hc_s, hc_r, hf_s, hf_r,
):
    tok, hd = q.shape
    tile = 256
    tiles = tok // tile
    piece = hd // PLANE

    z = lax.axis_index("z")
    yh = lax.axis_index("yh")
    x = lax.axis_index("x")
    yl = lax.axis_index("yl")
    c = lax.axis_index("c")
    seq = z * 8 + yh * 4 + x
    plane = z * 2 + yh
    head = yl * 2 + c

    def at_seq(by):
        there = lax.rem(seq + by % BLOCKS, BLOCKS)
        return {"z": there // 8, "yh": lax.rem(there, 8) // 4, "x": lax.rem(there, 4)}

    def at_x(by):
        return {"x": lax.rem(x + by % 4, 4)}

    def at_plane(by):
        there = lax.rem(plane + by, PLANE)
        return {"z": there // 2, "yh": lax.rem(there, 2)}

    chip = {"yl": 1 - yl}
    core = {"c": 1 - c}
    across = {"yl": 1 - yl, "c": 1 - c}

    def remote(src, dst, send, recv, where):
        return pltpu.make_async_remote_copy(
            src_ref=src, dst_ref=dst, send_sem=send, recv_sem=recv,
            device_id=where, device_id_type=MESH,
        )

    barrier = pltpu.get_barrier_semaphore()
    greeted = 0
    for where in (
        [at_seq(by) for by in (4, -4, 1, -1)]
        + [at_x(by) for by in (1, 2, 3)]
        + [chip, core, across]
    ):
        pl.semaphore_signal(barrier, inc=1, device_id=where, device_id_type=MESH)
        greeted += 1

    def greet(by, carry):
        pl.semaphore_signal(barrier, inc=1, device_id=at_plane(by), device_id_type=MESH)
        return carry

    lax.fori_loop(1, PLANE, greet, 0)
    pl.semaphore_wait(barrier, greeted + PLANE - 1)

    def rows(i):
        return pl.ds(i * tile, tile)

    own = (k, v)
    held = (kh, vh)

    def row_copy(kind, i):
        n = kind * tiles + i
        return remote(own[kind].at[rows(i)], held[kind].at[3, rows(i)], row_s.at[n], row_r.at[n], at_seq(4))

    def d1_copy(kind, i, first):
        n = kind * tiles + i
        src = own[kind].at[rows(i)] if first else held[kind].at[3, rows(i)]
        return remote(src, held[kind].at[0, rows(i)], d1_s.at[n], d1_r.at[n], at_x(1))

    def d3_copy(kind, i, first):
        n = kind * tiles + i
        src = own[kind].at[rows(i)] if first else held[kind].at[3, rows(i)]
        return remote(src, held[kind].at[2, rows(i)], d3_s.at[n], d3_r.at[n], at_x(-1))

    def d2_copy(kind, i):
        n = kind * tiles + i
        if kind == 0:
            return remote(kh.at[0, rows(i)], kh.at[1, rows(i)], d2_s.at[n], d2_r.at[n], at_seq(1))
        return remote(vh.at[2, rows(i)], vh.at[1, rows(i)], d2_s.at[n], d2_r.at[n], at_seq(-1))

    for kind in (1, 0):
        for i in range(tiles):
            row_copy(kind, i).start()

    @pl.when(x < 3)
    def _():
        for i in range(tiles):
            d1_copy(0, i, True).start()

    @pl.when(x == 0)
    def _():
        for i in range(tiles):
            d3_copy(1, i, True).start()

    def w_copy(n, where, there):
        cols = pl.ds(pl.multiple_of(there * hd, 128), hd)
        return remote(out_w.at[:, cols], wcol.at[head], w_s.at[n], w_r.at[n], where)

    w_copies = (
        w_copy(0, core, yl * 2 + 1 - c),
        w_copy(1, chip, (1 - yl) * 2 + c),
        w_copy(2, across, (1 - yl) * 2 + 1 - c),
    )
    for copy in w_copies:
        copy.start()

    rate = jnp.transpose(jnp.broadcast_to(lr[...], (128, tok)))
    total[...] = rate

    def grad_tile(i, carry):
        at = pl.ds(pl.multiple_of(i * tile, tile), tile)
        k_t = k[at, :]
        gate_k = dot_nn(k_t, weights[0])
        up_k = dot_nn(k_t, weights[1])
        sig = 1.0 / (1.0 + jnp.exp(-gate_k))
        hid[at, :] = (gate_k * sig * up_k).astype(BF16)
        slow = total[at, :]
        slow = jnp.concatenate([slow] * (hd // 128), axis=1)
        target = (-slow * v[at, :].astype(F32)).astype(BF16)
        tgt[at, :] = target
        back = dot_nt(target, weights[2])
        dgate[at, :] = (back * up_k * sig * (1.0 + gate_k * (1.0 - sig))).astype(BF16)
        dup[at, :] = (back * gate_k * sig).astype(BF16)
        return carry

    lax.fori_loop(0, tiles, grad_tile, 0)
    for m, (a, b) in enumerate(((k, dgate), (k, dup), (hid, tgt))):
        mine = dot_tn(a[...], b[...])
        part[m] = mine
        psend[m] = mine.astype(BF16)

    def xs_copy(by):
        m = lax.rem(x + 4 - by, 4)
        to = jnp.minimum(m, 2)
        return m, remote(psend.at[to], precv.at[by - 1], xs_s.at[by - 1], xs_r.at[by - 1], {"x": m})

    for by in (1, 2, 3):
        m, copy = xs_copy(by)

        @pl.when(m < 3)
        def _(copy=copy):
            copy.start()

    @pl.when(x < 3)
    def _():
        for i in range(tiles):
            d1_copy(1, i, True).start()

    @pl.when(x == 0)
    def _():
        for i in range(tiles):
            d3_copy(0, i, True).start()

    scale = log2_e * hd**-0.5

    def attend(keys, values, distance):
        def step(i, carry):
            at = pl.ds(pl.multiple_of(i * tile, tile), tile)
            scores = dot_nt(q[at, :], keys[...]) * scale
            if distance in (0, 4):
                row = lax.broadcasted_iota(jnp.int32, scores.shape, 0) + i * tile
                col = lax.broadcasted_iota(jnp.int32, scores.shape, 1)
                valid = col <= row if distance == 0 else col > row
                scores = jnp.where(valid, scores, big_negative)
            peak = jnp.max(scores, axis=1, keepdims=True)
            if distance == 0:
                expo = jnp.exp2(scores - peak)
                top[at, :] = jnp.broadcast_to(peak, (tile, 128))
                total[at, :] = jnp.broadcast_to(jnp.sum(expo, axis=1, keepdims=True), (tile, 128))
                acc[at, :] = dot_nn(expo.astype(BF16), values[...])
            else:
                old = top[at, :][:, :1]
                peak = jnp.maximum(peak, old)
                shrink = jnp.exp2(old - peak)
                expo = jnp.exp2(scores - peak)
                top[at, :] = jnp.broadcast_to(peak, (tile, 128))
                more = jnp.sum(expo, axis=1, keepdims=True)
                total[at, :] = total[at, :] * shrink + more
                acc[at, :] = acc[at, :] * shrink + dot_nn(expo.astype(BF16), values[...])
            return carry

        lax.fori_loop(0, tiles, step, 0)

    attend(k, v, 0)

    @pl.when(x > 0)
    def _():
        for i in range(tiles):
            d1_copy(0, i, True).wait_recv()
            d2_copy(0, i).start()

    def pass_on(kind):
        for i in range(tiles):
            row_copy(kind, i).wait_recv()

            @pl.when(x == 3)
            def _():
                d1_copy(kind, i, False).start()

            @pl.when(x > 0)
            def _():
                d3_copy(kind, i, False).start()

    pass_on(1)

    owner = x < 3
    which = jnp.minimum(x, 2)

    def zs_copy(by):
        to = lax.rem(plane + by, PLANE)
        return remote(zsend.at[to], zrecv.at[by - 1], zs_s.at[by - 1], zs_r.at[by - 1], at_plane(by))

    def ag_copy(by):
        return remote(zsum, grad.at[plane], ag_s.at[by - 1], ag_r.at[by - 1], at_plane(by))

    def each(fn):
        def go(by, carry):
            fn(by)
            return carry

        lax.fori_loop(1, PLANE, go, 0)

    @pl.when(owner)
    def _():
        for by in (1, 2, 3):
            xs_copy(by)[1].wait_recv()
        whole = part[which] + precv[0].astype(F32) + precv[1].astype(F32) + precv[2].astype(F32)
        zsend[...] = whole.reshape(PLANE, piece, hd)
        each(lambda by: zs_copy(by).start())

    for i in range(tiles):
        d3_copy(1, i, True).wait_recv()
        d2_copy(1, i).start()

    pass_on(0)

    @pl.when(seq >= 4)
    def _():
        attend(kh.at[3], vh.at[3], 4)

    @pl.when(owner)
    def _():
        each(lambda by: zs_copy(by).wait_recv())
        zsum[...] = jnp.sum(zrecv[...], axis=0) + zsend[plane]
        grad[plane] = zsum[...]
        each(lambda by: ag_copy(by).start())

    @pl.when(x == 0)
    def _():
        for i in range(tiles):
            d1_copy(0, i, True).wait_recv()
            d2_copy(0, i).start()

    for i in range(tiles):
        d1_copy(1, i, True).wait_recv()

    @pl.when(seq >= 1)
    def _():
        attend(kh.at[0], vh.at[0], 1)

    for i in range(tiles):
        d3_copy(0, i, True).wait_recv()

    @pl.when(seq >= 3)
    def _():
        attend(kh.at[2], vh.at[2], 3)

    def bc_copy(by):
        return remote(new.at[which], new.at[which], bc_s.at[by - 1], bc_r.at[which], at_x(by))

    @pl.when(owner)
    def _():
        def arrived(by):
            lag = lax.rem(plane + PLANE - by, PLANE)
            remote(zsum, grad.at[lag], ag_s.at[by - 1], ag_r.at[by - 1], at_plane(by)).wait_recv()

        each(arrived)
        whole = grad[...].reshape(hd, hd)
        norm = jnp.sqrt(jnp.sum(whole * whole)) + 1e-07
        part[0] = whole / norm

        def spread(wide):
            high, low = halves(wide)
            left[:, 0:hd] = high
            left[:, hd : 2 * hd] = low
            left[:, 2 * hd : 3 * hd] = high
            return high, low

        def spread_both(wide):
            high, low = spread(wide)
            right[:, 0:hd] = high
            right[:, hd : 2 * hd] = high
            right[:, 2 * hd : 3 * hd] = low
            return high, low

        def sweep(n, carry):
            high, low = spread_both(part[0])
            stack[0:hd] = high
            stack[hd : 2 * hd] = high
            stack[2 * hd : 3 * hd] = low
            square = dot_nt(left[...], right[...])
            part[1] = square
            spread_both(square)
            part[1] = ns_second * part[1] + ns_third * dot_nt(left[...], right[...])
            spread(part[1])
            part[0] = ns_first * part[0] + dot_nn(left[...], stack[...])
            return carry

        lax.fori_loop(0, 5, sweep, 0)
        new[which] = (weights[which].astype(F32) - part[0]).astype(BF16)
        for by in (1, 2, 3):
            bc_copy(by).start()

    for kind in (0, 1):
        for i in range(tiles):
            d2_copy(kind, i).wait_recv()

    @pl.when(seq >= 2)
    def _():
        attend(kh.at[1], vh.at[1], 2)

    for m in range(3):

        @pl.when(x != m)
        def _():
            remote(new.at[m], new.at[m], bc_s.at[0], bc_r.at[m], at_x(1)).wait_recv()

    def hy_copy(i):
        return remote(comb.at[head, rows(i)], comb.at[head, rows(i)], hy_s.at[i], hy_r.at[i], chip)

    def hc_copy(i):
        return remote(comb.at[head, rows(i)], comb.at[head, rows(i)], hc_s.at[i], hc_r.at[i], core)

    far = (1 - yl) * 2 + c

    def hf_copy(i):
        return remote(comb.at[far, rows(i)], comb.at[far, rows(i)], hf_s.at[i], hf_r.at[i], core)

    for i in range(tiles):
        at = rows(i)
        q_t = q[at, :]
        gate_q = dot_nn(q_t, new[0])
        up_q = dot_nn(q_t, new[1])
        q_hidden = (gate_q * (1.0 / (1.0 + jnp.exp(-gate_q))) * up_q).astype(BF16)
        fast = dot_nn(q_hidden, new[2])
        mean = jnp.mean(fast * fast, axis=1, keepdims=True)
        ttt = fast * lax.rsqrt(mean + 1e-06) * gain[...]
        attended = acc[at, :] / total[at, :][:, :1]
        comb[head, at, :] = (attended + ttt).astype(BF16)
        hy_copy(i).start()
        hc_copy(i).start()

    for i in range(tiles):
        hy_copy(i).wait_recv()
        hf_copy(i).start()

    for copy in w_copies:
        copy.wait()
    wcol[head] = out_w[:, pl.ds(pl.multiple_of(head * hd, 128), hd)]

    for i in range(tiles):
        hc_copy(i).wait_recv()
        hf_copy(i).wait_recv()
        at = rows(i)
        mixed = dot_nn(comb[0, at, :], wcol[0])
        for h in range(1, 4):
            mixed += dot_nn(comb[h, at, :], wcol[h])
        out[at, :] = mixed.astype(BF16)

    for kind in (0, 1):
        for i in range(tiles):
            row_copy(kind, i).wait_send()
            d1_copy(kind, i, True).wait_send()
            d2_copy(kind, i).wait_send()
            d3_copy(kind, i, True).wait_send()
    for by in (1, 2, 3):
        m, copy = xs_copy(by)

        @pl.when(m < 3)
        def _(copy=copy):
            copy.wait_send()

    @pl.when(owner)
    def _():
        each(lambda by: zs_copy(by).wait_send())
        each(lambda by: ag_copy(by).wait_send())
        for by in (1, 2, 3):
            bc_copy(by).wait_send()

    for i in range(tiles):
        hy_copy(i).wait_send()
        hc_copy(i).wait_send()
        hf_copy(i).wait_send()


def shards(queries, keys, values, learn_rate, gate_fast, up_fast, down_fast, ttt_gain, out_weight):
    tok, hd = queries.shape
    tiles = tok // 256
    weights = jnp.concatenate([gate_fast, up_fast, down_fast])
    piece = hd // PLANE
    dma = lambda n: pltpu.SemaphoreType.DMA((n,))
    scratch = [
        pltpu.VMEM((4, tok, hd), BF16),
        pltpu.VMEM((4, tok, hd), BF16),
        pltpu.VMEM((tok, hd), F32),
        pltpu.VMEM((tok, 128), F32),
        pltpu.VMEM((tok, 128), F32),
        pltpu.VMEM((tok, hd), BF16),
        pltpu.VMEM((tok, hd), BF16),
        pltpu.VMEM((tok, hd), BF16),
        pltpu.VMEM((tok, hd), BF16),
        pltpu.VMEM((3, hd, hd), F32),
        pltpu.VMEM((3, hd, hd), BF16),
        pltpu.VMEM((3, hd, hd), BF16),
        pltpu.VMEM((PLANE, piece, hd), F32),
        pltpu.VMEM((PLANE - 1, piece, hd), F32),
        pltpu.VMEM((piece, hd), F32),
        pltpu.VMEM((PLANE, piece, hd), F32),
        pltpu.VMEM((hd, 3 * hd), BF16),
        pltpu.VMEM((hd, 3 * hd), BF16),
        pltpu.VMEM((3 * hd, hd), BF16),
        pltpu.VMEM((3, hd, hd), BF16),
        pltpu.VMEM((4, tok, hd), BF16),
        pltpu.VMEM((4, hd, hd), BF16),
    ]
    scratch += [dma(2 * tiles)] * 8
    scratch += [dma(3)] * 2 + [dma(PLANE - 1)] * 4 + [dma(3)] * 2
    scratch += [dma(3)] * 2 + [dma(tiles)] * 6
    vmem = pl.BlockSpec(memory_space=pltpu.VMEM)
    return pl.pallas_call(
        layer,
        out_shape=jax.ShapeDtypeStruct((tok, hd), BF16),
        in_specs=[vmem] * 7,
        out_specs=vmem,
        scratch_shapes=scratch,
        compiler_params=pltpu.CompilerParams(
            collective_id=0, has_side_effects=True, vmem_limit_bytes=56 * 1024 * 1024
        ),
        name="layer",
    )(queries, keys, values, learn_rate, weights, ttt_gain, out_weight)


def solution(mesh):
    torus = Mesh(mesh.devices.reshape(SIZES), AXES)
    in_specs = (
        P(SEQ, HEAD),
        P(SEQ, HEAD),
        P(SEQ, HEAD),
        P(HEAD, SEQ),
        P(HEAD, None, None),
        P(HEAD, None, None),
        P(HEAD, None, None),
        P(HEAD, None),
        P(HEAD, None),
    )
    return jax.shard_map(
        shards, mesh=torus, in_specs=in_specs, out_specs=P(SEQ, HEAD), check_vma=False
    )
```

```python
import functools

import jax
import jax.numpy as jnp
from jax import lax
from jax.experimental import pallas as pl
from jax.experimental.pallas import tpu as pltpu
from jax.sharding import Mesh
from jax.sharding import PartitionSpec as P

AXES = ("z", "yh", "x", "yl", "c")
SIZES = (8, 2, 4, 2, 2)
SEQ = ("z", "yh", "x")
HEAD = ("yl", "c")
BLOCKS = 64
PLANE = 16
PARTS = 6
MESH = pl.DeviceIdType.MESH
BF16 = jnp.bfloat16
F32 = jnp.float32

ns_first = 3.4445
ns_second = -4.775
ns_third = 2.0315
big_negative = -1e30
log2_e = 1.4426950408889634


def dot_nn(left, right):
    return lax.dot_general(left, right, (((1,), (0,)), ((), ())), preferred_element_type=F32)


def dot_nt(left, right):
    return lax.dot_general(left, right, (((1,), (1,)), ((), ())), preferred_element_type=F32)


def dot_tn(left, right):
    return lax.dot_general(left, right, (((0,), (0,)), ((), ())), preferred_element_type=F32)


def halves(wide):
    high = wide.astype(BF16)
    low = (wide - high.astype(F32)).astype(BF16)
    return high, low


def layer(
    q, k, v, lr, gate_w, up_w, down_w, gain, out_w,
    out,
    kh, vh, acc, top, total,
    hid, tgt, dgate, dup, part, psend, precv,
    zsend, zrecv, zsum, grad, left, right, stack, new,
    comb, wcol,
    row_s, row_r, d1_s, d1_r, d2_s, d2_r, d3_s, d3_r, d4_s,
    xs_s, xs_r, zs_s, zs_r, ag_s, ag_r, bc_s, bc_r,
    w_s, w_r, hy_s, hy_r, hc_s, hc_r, hf_s, hf_r,
):
    tok, hd = q.shape
    tile = 256
    tiles = tok // tile
    chunk = tok // PARTS
    piece = hd // PLANE

    z = lax.axis_index("z")
    yh = lax.axis_index("yh")
    x = lax.axis_index("x")
    yl = lax.axis_index("yl")
    c = lax.axis_index("c")
    seq = z * 8 + yh * 4 + x
    plane = z * 2 + yh
    head = yl * 2 + c

    def at_seq(by):
        there = lax.rem(seq + by % BLOCKS, BLOCKS)
        return {"z": there // 8, "yh": lax.rem(there, 8) // 4, "x": lax.rem(there, 4)}

    def at_x(by):
        return {"x": lax.rem(x + by % 4, 4)}

    def at_plane(by):
        there = lax.rem(plane + by, PLANE)
        return {"z": there // 2, "yh": lax.rem(there, 2)}

    chip = {"yl": 1 - yl}
    core = {"c": 1 - c}
    across = {"yl": 1 - yl, "c": 1 - c}

    def remote(src, dst, send, recv, where):
        return pltpu.make_async_remote_copy(
            src_ref=src, dst_ref=dst, send_sem=send, recv_sem=recv,
            device_id=where, device_id_type=MESH,
        )

    barrier = pltpu.get_barrier_semaphore()
    greeted = 0
    for where in (
        [at_seq(by) for by in (4, -4, 1, -1)]
        + [at_x(by) for by in (1, 2, 3)]
        + [chip, core, across]
    ):
        pl.semaphore_signal(barrier, inc=1, device_id=where, device_id_type=MESH)
        greeted += 1

    def greet(by, carry):
        pl.semaphore_signal(barrier, inc=1, device_id=at_plane(by), device_id_type=MESH)
        return carry

    lax.fori_loop(1, PLANE, greet, 0)

    def rows(i):
        return pl.ds(i * tile, tile)

    def span(i):
        return pl.ds(i * chunk, chunk)

    own = (k, v)
    held = (kh, vh)

    def row_copy(kind, i):
        n = kind * PARTS + i
        return remote(own[kind].at[span(i)], held[kind].at[3, span(i)], row_s.at[n], row_r.at[n], at_seq(4))

    def d1_copy(kind, i, first):
        n = kind * PARTS + i
        src = own[kind].at[span(i)] if first else held[kind].at[3, span(i)]
        return remote(src, held[kind].at[0, span(i)], d1_s.at[n], d1_r.at[n], at_x(1))

    def d3_copy(kind, i, first):
        n = kind * PARTS + i
        src = own[kind].at[span(i)] if first else held[kind].at[3, span(i)]
        return remote(src, held[kind].at[2, span(i)], d3_s.at[n], d3_r.at[n], at_x(-1))

    def d2_copy(kind, i):
        n = kind * PARTS + i
        if kind == 0:
            return remote(kh.at[0, span(i)], kh.at[1, span(i)], d2_s.at[n], d2_r.at[n], at_seq(1))
        return remote(vh.at[2, span(i)], vh.at[1, span(i)], d2_s.at[n], d2_r.at[n], at_seq(-1))

    rate = jnp.transpose(jnp.broadcast_to(lr[...], (128, tok)))
    total[...] = rate

    def grad_tile(i, carry):
        at = pl.ds(pl.multiple_of(i * tile, tile), tile)
        k_t = k[at, :]
        gate_k = dot_nn(k_t, gate_w[0])
        up_k = dot_nn(k_t, up_w[0])
        sig = 1.0 / (1.0 + jnp.exp(-gate_k))
        hid[at, :] = (gate_k * sig * up_k).astype(BF16)
        slow = total[at, :]
        slow = jnp.concatenate([slow] * (hd // 128), axis=1)
        target = (-slow * v[at, :].astype(F32)).astype(BF16)
        tgt[at, :] = target
        back = dot_nt(target, down_w[0])
        dgate[at, :] = (back * up_k * sig * (1.0 + gate_k * (1.0 - sig))).astype(BF16)
        dup[at, :] = (back * gate_k * sig).astype(BF16)
        return carry

    lax.fori_loop(0, tiles, grad_tile, 0)
    for m, (a, b) in enumerate(((k, dgate), (k, dup), (hid, tgt))):
        mine = dot_tn(a[...], b[...])
        part[m] = mine
        psend[m] = mine.astype(BF16)

    scale = log2_e * hd**-0.5

    def attend(keys, values, distance):
        def step(i, carry):
            at = pl.ds(pl.multiple_of(i * tile, tile), tile)
            scores = dot_nt(q[at, :], keys[...]) * scale
            if distance in (0, 4):
                row = lax.broadcasted_iota(jnp.int32, scores.shape, 0) + i * tile
                col = lax.broadcasted_iota(jnp.int32, scores.shape, 1)
                valid = col <= row if distance == 0 else col > row
                scores = jnp.where(valid, scores, big_negative)
            peak = jnp.max(scores, axis=1, keepdims=True)
            if distance == 0:
                expo = jnp.exp2(scores - peak)
                top[at, :] = jnp.broadcast_to(peak, (tile, 128))
                total[at, :] = jnp.broadcast_to(jnp.sum(expo, axis=1, keepdims=True), (tile, 128))
                acc[at, :] = dot_nn(expo.astype(BF16), values[...])
            else:
                old = top[at, :][:, :1]
                peak = jnp.maximum(peak, old)
                shrink = jnp.exp2(old - peak)
                expo = jnp.exp2(scores - peak)
                top[at, :] = jnp.broadcast_to(peak, (tile, 128))
                more = jnp.sum(expo, axis=1, keepdims=True)
                total[at, :] = total[at, :] * shrink + more
                acc[at, :] = acc[at, :] * shrink + dot_nn(expo.astype(BF16), values[...])
            return carry

        lax.fori_loop(0, tiles, step, 0)

    def w_copy(n, where, there):
        cols = pl.ds(pl.multiple_of(there * hd, 128), hd)
        return remote(out_w.at[:, cols], wcol.at[head], w_s.at[n], w_r.at[n], where)

    w_copies = (
        w_copy(0, core, yl * 2 + 1 - c),
        w_copy(1, chip, (1 - yl) * 2 + c),
        w_copy(2, across, (1 - yl) * 2 + 1 - c),
    )
    attend(k, v, 0)

    def pass_on(kind, i):
        row_copy(kind, i).wait_recv()

        @pl.when(x == 3)
        def _():
            d1_copy(kind, i, False).start()

        @pl.when(x > 0)
        def _():
            d3_copy(kind, i, False).start()

    def send_keys(i):
        d1_copy(0, i, True).wait_recv()
        d2_copy(0, i).start()

    def send_values(i):
        d3_copy(1, i, True).wait_recv()

        @pl.when(x > 0)
        def _():
            d2_copy(1, i).start()

    def right_copy(i):
        return remote(vh.at[0, span(i)], vh.at[1, span(i)], d4_s.at[i], d2_r.at[PARTS + i], at_x(1))

    owner = x < 3
    which = jnp.minimum(x, 2)

    def xs_copy(by):
        m = lax.rem(x + 4 - by, 4)
        to = jnp.minimum(m, 2)
        return m, remote(psend.at[to], precv.at[by - 1], xs_s.at[by - 1], xs_r.at[by - 1], {"x": m})

    def zs_copy(by):
        to = lax.rem(plane + by, PLANE)
        return remote(zsend.at[to], zrecv.at[by - 1], zs_s.at[by - 1], zs_r.at[by - 1], at_plane(by))

    def ag_copy(by):
        return remote(zsum, grad.at[plane], ag_s.at[by - 1], ag_r.at[by - 1], at_plane(by))

    def each(fn):
        def go(by, carry):
            fn(by)
            return carry

        lax.fori_loop(1, PLANE, go, 0)

    pl.semaphore_wait(barrier, greeted + PLANE - 1)

    for by in (1, 2, 3):
        m, copy = xs_copy(by)

        @pl.when(m < 3)
        def _(copy=copy):
            copy.start()

    for kind in (1, 0):
        for i in range(PARTS):
            row_copy(kind, i).start()

    @pl.when(owner)
    def _():
        for by in (1, 2, 3):
            xs_copy(by)[1].wait_recv()
        whole = part[which] + precv[0].astype(F32) + precv[1].astype(F32) + precv[2].astype(F32)
        part[which] = whole
        zsend[...] = whole.reshape(PLANE, piece, hd).astype(BF16)
        each(lambda by: zs_copy(by).start())

    @pl.when(x < 3)
    def _():
        for kind in (0, 1):
            for i in range(PARTS):
                d1_copy(kind, i, True).start()

    @pl.when(x == 0)
    def _():
        for kind in (1, 0):
            for i in range(PARTS):
                d3_copy(kind, i, True).start()

    for i in range(PARTS):
        pass_on(1, i)
        if i >= 1:
            send_values(i - 1)

    send_values(PARTS - 1)

    @pl.when(x > 0)
    def _():
        for i in range(PARTS // 2):
            send_keys(i)

    for i in range(PARTS // 2):
        pass_on(0, i)

    @pl.when(x > 0)
    def _():
        for i in range(PARTS // 2, PARTS):
            send_keys(i)

    @pl.when(owner)
    def _():
        each(lambda by: zs_copy(by).wait_recv())
        first = pl.multiple_of(plane * piece, 8)
        zsum[...] = jnp.sum(zrecv[...].astype(F32), axis=0) + part[which, pl.ds(first, piece), :]
        grad[plane] = zsum[...]
        each(lambda by: ag_copy(by).start())

    for i in range(PARTS // 2, PARTS):
        pass_on(0, i)

    for copy in w_copies:
        copy.start()

    @pl.when(x == 2)
    def _():
        for i in range(PARTS):
            d1_copy(1, i, True).wait_recv()
            right_copy(i).start()

    @pl.when(x == 0)
    def _():
        for i in range(PARTS):
            send_keys(i)

    @pl.when(seq >= 4)
    def _():
        attend(kh.at[3], vh.at[3], 4)

    def bc_copy(by):
        return remote(new.at[which], new.at[which], bc_s.at[by - 1], bc_r.at[which], at_x(by))

    @pl.when(owner)
    def _():
        def arrived(by):
            lag = lax.rem(plane + PLANE - by, PLANE)
            remote(zsum, grad.at[lag], ag_s.at[by - 1], ag_r.at[by - 1], at_plane(by)).wait_recv()

        each(arrived)
        whole = grad[...].reshape(hd, hd)
        norm = jnp.sqrt(jnp.sum(whole * whole)) + 1e-07
        part[0] = whole / norm

        def spread(wide):
            high, low = halves(wide)
            left[:, 0:hd] = high
            left[:, hd : 2 * hd] = low
            left[:, 2 * hd : 3 * hd] = high
            return high, low

        def spread_both(wide):
            high, low = spread(wide)
            right[:, 0:hd] = high
            right[:, hd : 2 * hd] = high
            right[:, 2 * hd : 3 * hd] = low
            return high, low

        def sweep(n, carry):
            high, low = spread_both(part[0])
            stack[0:hd] = high
            stack[hd : 2 * hd] = high
            stack[2 * hd : 3 * hd] = low
            square = dot_nt(left[...], right[...])
            part[1] = square
            spread_both(square)
            part[1] = ns_second * part[1] + ns_third * dot_nt(left[...], right[...])
            spread(part[1])
            part[0] = ns_first * part[0] + dot_nn(left[...], stack[...])
            return carry

        lax.fori_loop(0, 5, sweep, 0)
        for m, old in enumerate((gate_w, up_w, down_w)):

            @pl.when(x == m)
            def _(m=m, old=old):
                new[m] = (old[0].astype(F32) - part[0]).astype(BF16)

        for by in (1, 2, 3):
            bc_copy(by).start()

    @pl.when(x != 2)
    def _():
        for i in range(PARTS):
            d1_copy(1, i, True).wait_recv()

    @pl.when(seq >= 1)
    def _():
        attend(kh.at[0], vh.at[0], 1)

    for i in range(PARTS):
        d3_copy(0, i, True).wait_recv()

    @pl.when(seq >= 3)
    def _():
        attend(kh.at[2], vh.at[2], 3)

    for kind in (0, 1):
        for i in range(PARTS):
            d2_copy(kind, i).wait_recv()

    @pl.when(seq >= 2)
    def _():
        attend(kh.at[1], vh.at[1], 2)

    for m in range(3):

        @pl.when(x != m)
        def _():
            remote(new.at[m], new.at[m], bc_s.at[0], bc_r.at[m], at_x(1)).wait_recv()

    def hy_copy(i):
        return remote(comb.at[head, rows(i)], comb.at[head, rows(i)], hy_s.at[i], hy_r.at[i], chip)

    def hc_copy(i):
        return remote(comb.at[head, rows(i)], comb.at[head, rows(i)], hc_s.at[i], hc_r.at[i], core)

    far = (1 - yl) * 2 + c

    def hf_copy(i):
        return remote(comb.at[far, rows(i)], comb.at[far, rows(i)], hf_s.at[i], hf_r.at[i], core)

    for i in range(tiles):
        at = rows(i)
        q_t = q[at, :]
        gate_q = dot_nn(q_t, new[0])
        up_q = dot_nn(q_t, new[1])
        q_hidden = (gate_q * (1.0 / (1.0 + jnp.exp(-gate_q))) * up_q).astype(BF16)
        fast = dot_nn(q_hidden, new[2])
        mean = jnp.mean(fast * fast, axis=1, keepdims=True)
        ttt = fast * lax.rsqrt(mean + 1e-06) * gain[...]
        attended = acc[at, :] / total[at, :][:, :1]
        comb[head, at, :] = (attended + ttt).astype(BF16)
        hy_copy(i).start()
        hc_copy(i).start()

    for i in range(tiles):
        hy_copy(i).wait_recv()
        hf_copy(i).start()

    for copy in w_copies:
        copy.wait()
    wcol[head] = out_w[:, pl.ds(pl.multiple_of(head * hd, 128), hd)]

    for i in range(tiles):
        hc_copy(i).wait_recv()
        hf_copy(i).wait_recv()
        at = rows(i)
        mixed = dot_nn(comb[0, at, :], wcol[0])
        for h in range(1, 4):
            mixed += dot_nn(comb[h, at, :], wcol[h])
        out[at, :] = mixed.astype(BF16)

    for kind in (0, 1):
        for i in range(PARTS):
            row_copy(kind, i).wait_send()
            d1_copy(kind, i, True).wait_send()
            d3_copy(kind, i, True).wait_send()
    for i in range(PARTS):
        d2_copy(0, i).wait_send()

        @pl.when(x > 0)
        def _():
            d2_copy(1, i).wait_send()

        @pl.when(x == 2)
        def _():
            right_copy(i).wait_send()
    for by in (1, 2, 3):
        m, copy = xs_copy(by)

        @pl.when(m < 3)
        def _(copy=copy):
            copy.wait_send()

    @pl.when(owner)
    def _():
        each(lambda by: zs_copy(by).wait_send())
        each(lambda by: ag_copy(by).wait_send())
        for by in (1, 2, 3):
            bc_copy(by).wait_send()

    for i in range(tiles):
        hy_copy(i).wait_send()
        hc_copy(i).wait_send()
        hf_copy(i).wait_send()


def shards(queries, keys, values, learn_rate, gate_fast, up_fast, down_fast, ttt_gain, out_weight):
    tok, hd = queries.shape
    tiles = tok // 256
    piece = hd // PLANE
    dma = lambda n: pltpu.SemaphoreType.DMA((n,))
    scratch = [
        pltpu.VMEM((4, tok, hd), BF16),
        pltpu.VMEM((4, tok, hd), BF16),
        pltpu.VMEM((tok, hd), F32),
        pltpu.VMEM((tok, 128), F32),
        pltpu.VMEM((tok, 128), F32),
        pltpu.VMEM((tok, hd), BF16),
        pltpu.VMEM((tok, hd), BF16),
        pltpu.VMEM((tok, hd), BF16),
        pltpu.VMEM((tok, hd), BF16),
        pltpu.VMEM((3, hd, hd), F32),
        pltpu.VMEM((3, hd, hd), BF16),
        pltpu.VMEM((3, hd, hd), BF16),
        pltpu.VMEM((PLANE, piece, hd), BF16),
        pltpu.VMEM((PLANE - 1, piece, hd), BF16),
        pltpu.VMEM((piece, hd), F32),
        pltpu.VMEM((PLANE, piece, hd), F32),
        pltpu.VMEM((hd, 3 * hd), BF16),
        pltpu.VMEM((hd, 3 * hd), BF16),
        pltpu.VMEM((3 * hd, hd), BF16),
        pltpu.VMEM((3, hd, hd), BF16),
        pltpu.VMEM((4, tok, hd), BF16),
        pltpu.VMEM((4, hd, hd), BF16),
    ]
    scratch += [dma(2 * PARTS)] * 8 + [dma(PARTS)]
    scratch += [dma(3)] * 2 + [dma(PLANE - 1)] * 4 + [dma(3)] * 2
    scratch += [dma(3)] * 2 + [dma(tiles)] * 6
    vmem = pl.BlockSpec(memory_space=pltpu.VMEM)
    return pl.pallas_call(
        layer,
        out_shape=jax.ShapeDtypeStruct((tok, hd), BF16),
        in_specs=[vmem] * 9,
        out_specs=vmem,
        scratch_shapes=scratch,
        compiler_params=pltpu.CompilerParams(
            collective_id=0, has_side_effects=True, vmem_limit_bytes=56 * 1024 * 1024
        ),
        name="layer",
    )(queries, keys, values, learn_rate, gate_fast, up_fast, down_fast, ttt_gain, out_weight)


def solution(mesh):
    torus = Mesh(mesh.devices.reshape(SIZES), AXES)
    in_specs = (
        P(SEQ, HEAD),
        P(SEQ, HEAD),
        P(SEQ, HEAD),
        P(HEAD, SEQ),
        P(HEAD, None, None),
        P(HEAD, None, None),
        P(HEAD, None, None),
        P(HEAD, None),
        P(HEAD, None),
    )
    return jax.shard_map(
        shards, mesh=torus, in_specs=in_specs, out_specs=P(SEQ, HEAD), check_vma=False
    )
```

```python
import functools

import jax
import jax.numpy as jnp
from jax import lax
from jax.experimental import pallas as pl
from jax.experimental.pallas import tpu as pltpu
from jax.sharding import Mesh
from jax.sharding import PartitionSpec as P

AXES = ("z", "yh", "x", "yl", "c")
SIZES = (8, 2, 4, 2, 2)
SEQ = ("z", "yh", "x")
HEAD = ("yl", "c")
BLOCKS = 64
PLANE = 16
PARTS = 6
MESH = pl.DeviceIdType.MESH
BF16 = jnp.bfloat16
F32 = jnp.float32

ns_first = 3.4445
ns_second = -4.775
ns_third = 2.0315
big_negative = -1e30
log2_e = 1.4426950408889634


def dot_nn(left, right):
    return lax.dot_general(left, right, (((1,), (0,)), ((), ())), preferred_element_type=F32)


def dot_nt(left, right):
    return lax.dot_general(left, right, (((1,), (1,)), ((), ())), preferred_element_type=F32)


def dot_tn(left, right):
    return lax.dot_general(left, right, (((0,), (0,)), ((), ())), preferred_element_type=F32)


def halves(wide):
    high = wide.astype(BF16)
    low = (wide - high.astype(F32)).astype(BF16)
    return high, low


def layer(
    q, k, v, lr, gate_w, up_w, down_w, gain, out_w,
    out,
    kh, vh, acc, top, total,
    hid, tgt, dgate, dup, part, psend, precv,
    zsend, zrecv, zsum, grad, left, right, stack, new,
    comb, wcol,
    row_s, row_r, d1_s, d1_r, d2_s, d2_r, d3_s, d3_r, d4_s,
    xs_s, xs_r, zs_s, zs_r, ag_s, ag_r, bc_s, bc_r,
    w_s, w_r, hy_s, hy_r, hc_s, hc_r, hf_s, hf_r,
):
    tok, hd = q.shape
    tile = 256
    tiles = tok // tile
    chunk = tok // PARTS
    piece = hd // PLANE

    z = lax.axis_index("z")
    yh = lax.axis_index("yh")
    x = lax.axis_index("x")
    yl = lax.axis_index("yl")
    c = lax.axis_index("c")
    seq = z * 8 + yh * 4 + x
    plane = z * 2 + yh
    head = yl * 2 + c

    def at_seq(by):
        there = lax.rem(seq + by % BLOCKS, BLOCKS)
        return {"z": there // 8, "yh": lax.rem(there, 8) // 4, "x": lax.rem(there, 4)}

    def at_x(by):
        return {"x": lax.rem(x + by % 4, 4)}

    def at_plane(by):
        there = lax.rem(plane + by, PLANE)
        return {"z": there // 2, "yh": lax.rem(there, 2)}

    chip = {"yl": 1 - yl}
    core = {"c": 1 - c}
    across = {"yl": 1 - yl, "c": 1 - c}

    def remote(src, dst, send, recv, where):
        return pltpu.make_async_remote_copy(
            src_ref=src, dst_ref=dst, send_sem=send, recv_sem=recv,
            device_id=where, device_id_type=MESH,
        )

    barrier = pltpu.get_barrier_semaphore()
    greeted = 0
    for where in (
        [at_seq(by) for by in (4, -4, 1, -1)]
        + [at_x(by) for by in (1, 2, 3)]
        + [chip, core, across]
    ):
        pl.semaphore_signal(barrier, inc=1, device_id=where, device_id_type=MESH)
        greeted += 1

    def greet(by, carry):
        pl.semaphore_signal(barrier, inc=1, device_id=at_plane(by), device_id_type=MESH)
        return carry

    lax.fori_loop(1, PLANE, greet, 0)

    def rows(i):
        return pl.ds(i * tile, tile)

    def span(i):
        return pl.ds(i * chunk if isinstance(i, int) else pl.multiple_of(i * chunk, chunk), chunk)

    own = (k, v)
    held = (kh, vh)

    def row_copy(kind, i):
        n = kind * PARTS + i
        return remote(own[kind].at[span(i)], held[kind].at[3, span(i)], row_s.at[n], row_r.at[n], at_seq(4))

    def d1_copy(kind, i, first):
        n = kind * PARTS + i
        src = own[kind].at[span(i)] if first else held[kind].at[3, span(i)]
        return remote(src, held[kind].at[0, span(i)], d1_s.at[n], d1_r.at[n], at_x(1))

    def d3_copy(kind, i, first):
        n = kind * PARTS + i
        src = own[kind].at[span(i)] if first else held[kind].at[3, span(i)]
        return remote(src, held[kind].at[2, span(i)], d3_s.at[n], d3_r.at[n], at_x(-1))

    def d2_copy(kind, i):
        n = kind * PARTS + i
        if kind == 0:
            return remote(kh.at[0, span(i)], kh.at[1, span(i)], d2_s.at[n], d2_r.at[n], at_seq(1))
        return remote(vh.at[2, span(i)], vh.at[1, span(i)], d2_s.at[n], d2_r.at[n], at_seq(-1))

    rate = jnp.transpose(jnp.broadcast_to(lr[...], (128, tok)))
    total[...] = rate

    def grad_tile(i, carry):
        at = pl.ds(pl.multiple_of(i * tile, tile), tile)
        k_t = k[at, :]
        gate_k = dot_nn(k_t, gate_w[0])
        up_k = dot_nn(k_t, up_w[0])
        sig = 1.0 / (1.0 + jnp.exp(-gate_k))
        hid[at, :] = (gate_k * sig * up_k).astype(BF16)
        slow = total[at, :]
        slow = jnp.concatenate([slow] * (hd // 128), axis=1)
        target = (-slow * v[at, :].astype(F32)).astype(BF16)
        tgt[at, :] = target
        back = dot_nt(target, down_w[0])
        dgate[at, :] = (back * up_k * sig * (1.0 + gate_k * (1.0 - sig))).astype(BF16)
        dup[at, :] = (back * gate_k * sig).astype(BF16)
        return carry

    lax.fori_loop(0, tiles, grad_tile, 0)
    for m, (a, b) in enumerate(((k, dgate), (k, dup), (hid, tgt))):
        mine = dot_tn(a[...], b[...])
        part[m] = mine
        psend[m] = mine.astype(BF16)

    scale = log2_e * hd**-0.5

    def attend(keys, values, distance):
        def step(i, carry):
            at = pl.ds(pl.multiple_of(i * tile, tile), tile)
            scores = dot_nt(q[at, :], keys[...]) * scale
            if distance in (0, 4):
                row = lax.broadcasted_iota(jnp.int32, scores.shape, 0) + i * tile
                col = lax.broadcasted_iota(jnp.int32, scores.shape, 1)
                valid = col <= row if distance == 0 else col > row
                scores = jnp.where(valid, scores, big_negative)
            peak = jnp.max(scores, axis=1, keepdims=True)
            if distance == 0:
                expo = jnp.exp2(scores - peak)
                top[at, :] = jnp.broadcast_to(peak, (tile, 128))
                total[at, :] = jnp.broadcast_to(jnp.sum(expo, axis=1, keepdims=True), (tile, 128))
                acc[at, :] = dot_nn(expo.astype(BF16), values[...])
            else:
                old = top[at, :][:, :1]
                peak = jnp.maximum(peak, old)
                shrink = jnp.exp2(old - peak)
                expo = jnp.exp2(scores - peak)
                top[at, :] = jnp.broadcast_to(peak, (tile, 128))
                more = jnp.sum(expo, axis=1, keepdims=True)
                total[at, :] = total[at, :] * shrink + more
                acc[at, :] = acc[at, :] * shrink + dot_nn(expo.astype(BF16), values[...])
            return carry

        lax.fori_loop(0, tiles, step, 0)

    def w_copy(n, where, there):
        cols = pl.ds(pl.multiple_of(there * hd, 128), hd)
        return remote(out_w.at[:, cols], wcol.at[head], w_s.at[n], w_r.at[n], where)

    w_copies = (
        w_copy(0, core, yl * 2 + 1 - c),
        w_copy(1, chip, (1 - yl) * 2 + c),
        w_copy(2, across, (1 - yl) * 2 + 1 - c),
    )
    attend(k, v, 0)

    def pass_on(kind, i):
        row_copy(kind, i).wait_recv()

        @pl.when(x == 3)
        def _():
            d1_copy(kind, i, False).start()

        @pl.when(x > 0)
        def _():
            d3_copy(kind, i, False).start()

    def send_keys(i):
        d1_copy(0, i, True).wait_recv()
        d2_copy(0, i).start()

    def send_values(i):
        d3_copy(1, i, True).wait_recv()

        @pl.when(x > 0)
        def _():
            d2_copy(1, i).start()

    def right_copy(i):
        return remote(vh.at[0, span(i)], vh.at[1, span(i)], d4_s.at[i], d2_r.at[PARTS + i], at_x(1))

    owner = x < 3
    which = jnp.minimum(x, 2)

    def xs_copy(by):
        m = lax.rem(x + 4 - by, 4)
        to = jnp.minimum(m, 2)
        return m, remote(psend.at[to], precv.at[by - 1], xs_s.at[by - 1], xs_r.at[by - 1], {"x": m})

    def zs_copy(by):
        to = lax.rem(plane + by, PLANE)
        return remote(zsend.at[to], zrecv.at[by - 1], zs_s.at[by - 1], zs_r.at[by - 1], at_plane(by))

    def ag_copy(by):
        return remote(zsum, grad.at[plane], ag_s.at[by - 1], ag_r.at[by - 1], at_plane(by))

    def each(fn):
        def go(by, carry):
            fn(by)
            return carry

        lax.fori_loop(1, PLANE, go, 0)

    pl.semaphore_wait(barrier, greeted + PLANE - 1)

    for by in (1, 2, 3):
        m, copy = xs_copy(by)

        @pl.when(m < 3)
        def _(copy=copy):
            copy.start()

    for kind in (1, 0):
        for i in range(PARTS):
            row_copy(kind, i).start()

    @pl.when(x == 2)
    def _():
        for kind in (0, 1):
            for i in range(PARTS):
                d1_copy(kind, i, True).start()

    @pl.when(owner)
    def _():
        for by in (1, 2, 3):
            xs_copy(by)[1].wait_recv()
        whole = part[which] + precv[0].astype(F32) + precv[1].astype(F32) + precv[2].astype(F32)
        part[which] = whole
        zsend[...] = whole.reshape(PLANE, piece, hd).astype(BF16)
        each(lambda by: zs_copy(by).start())

    @pl.when(x < 2)
    def _():
        for kind in (0, 1):
            for i in range(PARTS):
                d1_copy(kind, i, True).start()

    @pl.when(x == 0)
    def _():
        for kind in (1, 0):
            for i in range(PARTS):
                d3_copy(kind, i, True).start()

    for i in range(PARTS):
        pass_on(1, i)
        if i >= 1:
            send_values(i - 1)

    send_values(PARTS - 1)

    @pl.when(x > 0)
    def _():
        for i in range(PARTS // 2):
            send_keys(i)

    for i in range(PARTS // 2):
        pass_on(0, i)

    @pl.when(x > 0)
    def _():
        for i in range(PARTS // 2, PARTS):
            send_keys(i)

    @pl.when(owner)
    def _():
        each(lambda by: zs_copy(by).wait_recv())
        first = pl.multiple_of(plane * piece, 8)
        zsum[...] = jnp.sum(zrecv[...].astype(F32), axis=0) + part[which, pl.ds(first, piece), :]
        grad[plane] = zsum[...]
        each(lambda by: ag_copy(by).start())

    for i in range(PARTS // 2, PARTS):
        pass_on(0, i)

    for copy in w_copies:
        copy.start()

    def send_right(i):
        d1_copy(1, i, True).wait_recv()
        right_copy(i).start()

    @pl.when(x == 2)
    def _():
        send_right(0)

    @pl.when(x == 0)
    def _():
        for i in range(PARTS):
            send_keys(i)

    def bc_copy(by):
        return remote(new.at[which], new.at[which], bc_s.at[by - 1], bc_r.at[which], at_x(by))

    @pl.when(owner)
    def _():
        def arrived(by):
            lag = lax.rem(plane + PLANE - by, PLANE)
            remote(zsum, grad.at[lag], ag_s.at[by - 1], ag_r.at[by - 1], at_plane(by)).wait_recv()

        each(arrived)
        whole = grad[...].reshape(hd, hd)
        norm = jnp.sqrt(jnp.sum(whole * whole)) + 1e-07
        part[0] = whole / norm

        def spread(wide):
            high, low = halves(wide)
            left[:, 0:hd] = high
            left[:, hd : 2 * hd] = low
            left[:, 2 * hd : 3 * hd] = high
            return high, low

        def spread_both(wide):
            high, low = spread(wide)
            right[:, 0:hd] = high
            right[:, hd : 2 * hd] = high
            right[:, 2 * hd : 3 * hd] = low
            return high, low

        def sweep(n, carry):
            high, low = spread_both(part[0])
            stack[0:hd] = high
            stack[hd : 2 * hd] = high
            stack[2 * hd : 3 * hd] = low
            square = dot_nt(left[...], right[...])
            part[1] = square
            spread_both(square)
            part[1] = ns_second * part[1] + ns_third * dot_nt(left[...], right[...])
            spread(part[1])
            part[0] = ns_first * part[0] + dot_nn(left[...], stack[...])

            @pl.when(x == 2)
            def _():
                send_right(n + 1)

            return carry

        lax.fori_loop(0, 5, sweep, 0)
        for m, old in enumerate((gate_w, up_w, down_w)):

            @pl.when(x == m)
            def _(m=m, old=old):
                new[m] = (old[0].astype(F32) - part[0]).astype(BF16)

        for by in (1, 2, 3):
            bc_copy(by).start()

    @pl.when(seq >= 4)
    def _():
        attend(kh.at[3], vh.at[3], 4)

    @pl.when(x != 2)
    def _():
        for i in range(PARTS):
            d1_copy(1, i, True).wait_recv()

    @pl.when(seq >= 1)
    def _():
        attend(kh.at[0], vh.at[0], 1)

    for i in range(PARTS):
        d3_copy(0, i, True).wait_recv()

    @pl.when(seq >= 3)
    def _():
        attend(kh.at[2], vh.at[2], 3)

    for kind in (0, 1):
        for i in range(PARTS):
            d2_copy(kind, i).wait_recv()

    @pl.when(seq >= 2)
    def _():
        attend(kh.at[1], vh.at[1], 2)

    for m in range(3):

        @pl.when(x != m)
        def _():
            remote(new.at[m], new.at[m], bc_s.at[0], bc_r.at[m], at_x(1)).wait_recv()

    def hy_copy(i):
        return remote(comb.at[head, rows(i)], comb.at[head, rows(i)], hy_s.at[i], hy_r.at[i], chip)

    def hc_copy(i):
        return remote(comb.at[head, rows(i)], comb.at[head, rows(i)], hc_s.at[i], hc_r.at[i], core)

    far = (1 - yl) * 2 + c

    def hf_copy(i):
        return remote(comb.at[far, rows(i)], comb.at[far, rows(i)], hf_s.at[i], hf_r.at[i], core)

    for i in range(tiles):
        at = rows(i)
        q_t = q[at, :]
        gate_q = dot_nn(q_t, new[0])
        up_q = dot_nn(q_t, new[1])
        q_hidden = (gate_q * (1.0 / (1.0 + jnp.exp(-gate_q))) * up_q).astype(BF16)
        fast = dot_nn(q_hidden, new[2])
        mean = jnp.mean(fast * fast, axis=1, keepdims=True)
        ttt = fast * lax.rsqrt(mean + 1e-06) * gain[...]
        attended = acc[at, :] / total[at, :][:, :1]
        comb[head, at, :] = (attended + ttt).astype(BF16)
        hy_copy(i).start()
        hc_copy(i).start()

    for i in range(tiles):
        hy_copy(i).wait_recv()
        hf_copy(i).start()

    for copy in w_copies:
        copy.wait()
    wcol[head] = out_w[:, pl.ds(pl.multiple_of(head * hd, 128), hd)]

    for i in range(tiles):
        hc_copy(i).wait_recv()
        hf_copy(i).wait_recv()
        at = rows(i)
        mixed = dot_nn(comb[0, at, :], wcol[0])
        for h in range(1, 4):
            mixed += dot_nn(comb[h, at, :], wcol[h])
        out[at, :] = mixed.astype(BF16)

    for kind in (0, 1):
        for i in range(PARTS):
            row_copy(kind, i).wait_send()
            d1_copy(kind, i, True).wait_send()
            d3_copy(kind, i, True).wait_send()
    for i in range(PARTS):
        d2_copy(0, i).wait_send()

        @pl.when(x > 0)
        def _():
            d2_copy(1, i).wait_send()

        @pl.when(x == 2)
        def _():
            right_copy(i).wait_send()
    for by in (1, 2, 3):
        m, copy = xs_copy(by)

        @pl.when(m < 3)
        def _(copy=copy):
            copy.wait_send()

    @pl.when(owner)
    def _():
        each(lambda by: zs_copy(by).wait_send())
        each(lambda by: ag_copy(by).wait_send())
        for by in (1, 2, 3):
            bc_copy(by).wait_send()

    for i in range(tiles):
        hy_copy(i).wait_send()
        hc_copy(i).wait_send()
        hf_copy(i).wait_send()


def shards(queries, keys, values, learn_rate, gate_fast, up_fast, down_fast, ttt_gain, out_weight):
    tok, hd = queries.shape
    tiles = tok // 256
    piece = hd // PLANE
    dma = lambda n: pltpu.SemaphoreType.DMA((n,))
    scratch = [
        pltpu.VMEM((4, tok, hd), BF16),
        pltpu.VMEM((4, tok, hd), BF16),
        pltpu.VMEM((tok, hd), F32),
        pltpu.VMEM((tok, 128), F32),
        pltpu.VMEM((tok, 128), F32),
        pltpu.VMEM((tok, hd), BF16),
        pltpu.VMEM((tok, hd), BF16),
        pltpu.VMEM((tok, hd), BF16),
        pltpu.VMEM((tok, hd), BF16),
        pltpu.VMEM((3, hd, hd), F32),
        pltpu.VMEM((3, hd, hd), BF16),
        pltpu.VMEM((3, hd, hd), BF16),
        pltpu.VMEM((PLANE, piece, hd), BF16),
        pltpu.VMEM((PLANE - 1, piece, hd), BF16),
        pltpu.VMEM((piece, hd), F32),
        pltpu.VMEM((PLANE, piece, hd), F32),
        pltpu.VMEM((hd, 3 * hd), BF16),
        pltpu.VMEM((hd, 3 * hd), BF16),
        pltpu.VMEM((3 * hd, hd), BF16),
        pltpu.VMEM((3, hd, hd), BF16),
        pltpu.VMEM((4, tok, hd), BF16),
        pltpu.VMEM((4, hd, hd), BF16),
    ]
    scratch += [dma(2 * PARTS)] * 8 + [dma(PARTS)]
    scratch += [dma(3)] * 2 + [dma(PLANE - 1)] * 4 + [dma(3)] * 2
    scratch += [dma(3)] * 2 + [dma(tiles)] * 6
    vmem = pl.BlockSpec(memory_space=pltpu.VMEM)
    return pl.pallas_call(
        layer,
        out_shape=jax.ShapeDtypeStruct((tok, hd), BF16),
        in_specs=[vmem] * 9,
        out_specs=vmem,
        scratch_shapes=scratch,
        compiler_params=pltpu.CompilerParams(
            collective_id=0, has_side_effects=True, vmem_limit_bytes=56 * 1024 * 1024
        ),
        name="layer",
    )(queries, keys, values, learn_rate, gate_fast, up_fast, down_fast, ttt_gain, out_weight)


def solution(mesh):
    torus = Mesh(mesh.devices.reshape(SIZES), AXES)
    in_specs = (
        P(SEQ, HEAD),
        P(SEQ, HEAD),
        P(SEQ, HEAD),
        P(HEAD, SEQ),
        P(HEAD, None, None),
        P(HEAD, None, None),
        P(HEAD, None, None),
        P(HEAD, None),
        P(HEAD, None),
    )
    return jax.shard_map(
        shards, mesh=torus, in_specs=in_specs, out_specs=P(SEQ, HEAD), check_vma=False
    )
```

```python
import functools

import jax
import jax.numpy as jnp
from jax import lax
from jax.experimental import pallas as pl
from jax.experimental.pallas import tpu as pltpu
from jax.sharding import Mesh
from jax.sharding import PartitionSpec as P

AXES = ("z", "yh", "x", "yl", "c")
SIZES = (8, 2, 4, 2, 2)
SEQ = ("z", "yh", "x")
HEAD = ("yl", "c")
BLOCKS = 64
PLANE = 16
PARTS = 6
MESH = pl.DeviceIdType.MESH
BF16 = jnp.bfloat16
F32 = jnp.float32

ns_first = 3.4445
ns_second = -4.775
ns_third = 2.0315
big_negative = -1e30
log2_e = 1.4426950408889634


def dot_nn(left, right):
    return lax.dot_general(left, right, (((1,), (0,)), ((), ())), preferred_element_type=F32)


def dot_nt(left, right):
    return lax.dot_general(left, right, (((1,), (1,)), ((), ())), preferred_element_type=F32)


def dot_tn(left, right):
    return lax.dot_general(left, right, (((0,), (0,)), ((), ())), preferred_element_type=F32)


def halves(wide):
    high = wide.astype(BF16)
    low = (wide - high.astype(F32)).astype(BF16)
    return high, low


def layer(
    q, k, v, lr, gate_w, up_w, down_w, gain, out_w,
    out,
    kh, vh, acc, top, total,
    hid, tgt, dgate, dup, part, psend, precv,
    zsend, zrecv, zsum, grad, left, right, stack, new,
    comb, wcol,
    row_s, row_r, d1_s, d1_r, d2_s, d2_r, d3_s, d3_r, d4_s,
    xs_s, xs_r, zs_s, zs_r, ag_s, ag_r, bc_s, bc_r,
    w_s, w_r, hy_s, hy_r, hc_s, hc_r, hf_s, hf_r,
):
    tok, hd = q.shape
    tile = 256
    tiles = tok // tile
    chunk = tok // PARTS
    piece = hd // PLANE

    z = lax.axis_index("z")
    yh = lax.axis_index("yh")
    x = lax.axis_index("x")
    yl = lax.axis_index("yl")
    c = lax.axis_index("c")
    seq = z * 8 + yh * 4 + x
    plane = z * 2 + yh
    head = yl * 2 + c

    def at_seq(by):
        there = lax.rem(seq + by % BLOCKS, BLOCKS)
        return {"z": there // 8, "yh": lax.rem(there, 8) // 4, "x": lax.rem(there, 4)}

    def at_x(by):
        return {"x": lax.rem(x + by % 4, 4)}

    def at_plane(by):
        there = lax.rem(plane + by, PLANE)
        return {"z": there // 2, "yh": lax.rem(there, 2)}

    chip = {"yl": 1 - yl}
    core = {"c": 1 - c}
    across = {"yl": 1 - yl, "c": 1 - c}

    def remote(src, dst, send, recv, where):
        return pltpu.make_async_remote_copy(
            src_ref=src, dst_ref=dst, send_sem=send, recv_sem=recv,
            device_id=where, device_id_type=MESH,
        )

    barrier = pltpu.get_barrier_semaphore()
    greeted = 0
    for where in (
        [at_seq(by) for by in (4, -4, 1, -1)]
        + [at_x(by) for by in (1, 2, 3)]
        + [chip, core, across]
    ):
        pl.semaphore_signal(barrier, inc=1, device_id=where, device_id_type=MESH)
        greeted += 1

    def greet(by, carry):
        pl.semaphore_signal(barrier, inc=1, device_id=at_plane(by), device_id_type=MESH)
        return carry

    lax.fori_loop(1, PLANE, greet, 0)

    def rows(i):
        return pl.ds(i * tile, tile)

    def span(i):
        return pl.ds(i * chunk if isinstance(i, int) else pl.multiple_of(i * chunk, chunk), chunk)

    own = (k, v)
    held = (kh, vh)

    def row_copy(kind, i):
        n = kind * PARTS + i
        return remote(own[kind].at[span(i)], held[kind].at[3, span(i)], row_s.at[n], row_r.at[n], at_seq(4))

    def d1_copy(kind, i, first):
        n = kind * PARTS + i
        src = own[kind].at[span(i)] if first else held[kind].at[3, span(i)]
        return remote(src, held[kind].at[0, span(i)], d1_s.at[n], d1_r.at[n], at_x(1))

    def d3_copy(kind, i, first):
        n = kind * PARTS + i
        src = own[kind].at[span(i)] if first else held[kind].at[3, span(i)]
        return remote(src, held[kind].at[2, span(i)], d3_s.at[n], d3_r.at[n], at_x(-1))

    def d2_copy(kind, i):
        n = kind * PARTS + i
        if kind == 0:
            return remote(kh.at[0, span(i)], kh.at[1, span(i)], d2_s.at[n], d2_r.at[n], at_seq(1))
        return remote(vh.at[2, span(i)], vh.at[1, span(i)], d2_s.at[n], d2_r.at[n], at_seq(-1))

    rate = jnp.transpose(jnp.broadcast_to(lr[...], (128, tok)))
    total[...] = rate

    def grad_tile(i, carry):
        at = pl.ds(pl.multiple_of(i * tile, tile), tile)
        k_t = k[at, :]
        gate_k = dot_nn(k_t, gate_w[0])
        up_k = dot_nn(k_t, up_w[0])
        sig = 1.0 / (1.0 + jnp.exp(-gate_k))
        hid[at, :] = (gate_k * sig * up_k).astype(BF16)
        slow = total[at, :]
        slow = jnp.concatenate([slow] * (hd // 128), axis=1)
        target = (-slow * v[at, :].astype(F32)).astype(BF16)
        tgt[at, :] = target
        back = dot_nt(target, down_w[0])
        dgate[at, :] = (back * up_k * sig * (1.0 + gate_k * (1.0 - sig))).astype(BF16)
        dup[at, :] = (back * gate_k * sig).astype(BF16)
        return carry

    lax.fori_loop(0, tiles, grad_tile, 0)
    for m, (a, b) in enumerate(((k, dgate), (k, dup), (hid, tgt))):
        mine = dot_tn(a[...], b[...])
        part[m] = mine
        psend[m] = mine.astype(BF16)

    scale = log2_e * hd**-0.5

    def attend(keys, values, distance):
        def step(i, carry):
            at = pl.ds(pl.multiple_of(i * tile, tile), tile)
            scores = dot_nt(q[at, :], keys[...]) * scale
            if distance in (0, 4):
                row = lax.broadcasted_iota(jnp.int32, scores.shape, 0) + i * tile
                col = lax.broadcasted_iota(jnp.int32, scores.shape, 1)
                valid = col <= row if distance == 0 else col > row
                scores = jnp.where(valid, scores, big_negative)
            peak = jnp.max(scores, axis=1, keepdims=True)
            if distance == 0:
                expo = jnp.exp2(scores - peak)
                top[at, :] = jnp.broadcast_to(peak, (tile, 128))
                total[at, :] = jnp.broadcast_to(jnp.sum(expo, axis=1, keepdims=True), (tile, 128))
                acc[at, :] = dot_nn(expo.astype(BF16), values[...])
            else:
                old = top[at, :][:, :1]
                peak = jnp.maximum(peak, old)
                shrink = jnp.exp2(old - peak)
                expo = jnp.exp2(scores - peak)
                top[at, :] = jnp.broadcast_to(peak, (tile, 128))
                more = jnp.sum(expo, axis=1, keepdims=True)
                total[at, :] = total[at, :] * shrink + more
                acc[at, :] = acc[at, :] * shrink + dot_nn(expo.astype(BF16), values[...])
            return carry

        lax.fori_loop(0, tiles, step, 0)

    def w_copy(n, where, there):
        cols = pl.ds(pl.multiple_of(there * hd, 128), hd)
        return remote(out_w.at[:, cols], wcol.at[head], w_s.at[n], w_r.at[n], where)

    w_copies = (
        w_copy(0, core, yl * 2 + 1 - c),
        w_copy(1, chip, (1 - yl) * 2 + c),
        w_copy(2, across, (1 - yl) * 2 + 1 - c),
    )
    attend(k, v, 0)

    def pass_on(kind, i):
        row_copy(kind, i).wait_recv()

        @pl.when(x == 3)
        def _():
            d1_copy(kind, i, False).start()

        @pl.when(x > 0)
        def _():
            d3_copy(kind, i, False).start()

    def send_keys(i):
        d1_copy(0, i, True).wait_recv()
        d2_copy(0, i).start()

    def send_values(i):
        d3_copy(1, i, True).wait_recv()

        @pl.when(x > 0)
        def _():
            d2_copy(1, i).start()

    def right_copy(i):
        return remote(vh.at[0, span(i)], vh.at[1, span(i)], d4_s.at[i], d2_r.at[PARTS + i], at_x(1))

    owner = x < 3
    which = jnp.minimum(x, 2)

    def xs_copy(by):
        m = lax.rem(x + 4 - by, 4)
        to = jnp.minimum(m, 2)
        return m, remote(psend.at[to], precv.at[by - 1], xs_s.at[by - 1], xs_r.at[by - 1], {"x": m})

    def zs_copy(by):
        to = lax.rem(plane + by, PLANE)
        return remote(zsend.at[to], zrecv.at[by - 1], zs_s.at[by - 1], zs_r.at[by - 1], at_plane(by))

    def ag_copy(by):
        return remote(zsum, grad.at[plane], ag_s.at[by - 1], ag_r.at[by - 1], at_plane(by))

    def each(fn):
        def go(n, carry):
            fn(lax.rem(n + PLANE // 2 - 2, PLANE - 1) + 1)
            return carry

        lax.fori_loop(1, PLANE, go, 0)

    pl.semaphore_wait(barrier, greeted + PLANE - 1)

    for by in (1, 2, 3):
        m, copy = xs_copy(by)

        @pl.when(m < 3)
        def _(copy=copy):
            copy.start()

    for kind in (1, 0):
        for i in range(PARTS):
            row_copy(kind, i).start()

    @pl.when(x == 2)
    def _():
        for kind in (0, 1):
            for i in range(PARTS):
                d1_copy(kind, i, True).start()

    @pl.when(owner)
    def _():
        for by in (1, 2, 3):
            xs_copy(by)[1].wait_recv()
        whole = part[which] + precv[0].astype(F32) + precv[1].astype(F32) + precv[2].astype(F32)
        part[which] = whole
        zsend[...] = whole.reshape(PLANE, piece, hd).astype(BF16)
        each(lambda by: zs_copy(by).start())

    @pl.when(x < 2)
    def _():
        for kind in (0, 1):
            for i in range(PARTS):
                d1_copy(kind, i, True).start()

    @pl.when(x == 0)
    def _():
        for kind in (1, 0):
            for i in range(PARTS):
                d3_copy(kind, i, True).start()

    for i in range(PARTS):
        pass_on(1, i)
        if i >= 1:
            send_values(i - 1)

    send_values(PARTS - 1)

    @pl.when(x > 0)
    def _():
        for i in range(PARTS // 2):
            send_keys(i)

    for i in range(PARTS // 2):
        pass_on(0, i)

    @pl.when(x > 0)
    def _():
        for i in range(PARTS // 2, PARTS):
            send_keys(i)

    @pl.when(owner)
    def _():
        each(lambda by: zs_copy(by).wait_recv())
        first = pl.multiple_of(plane * piece, 8)
        zsum[...] = jnp.sum(zrecv[...].astype(F32), axis=0) + part[which, pl.ds(first, piece), :]
        grad[plane] = zsum[...]
        each(lambda by: ag_copy(by).start())

    for i in range(PARTS // 2, PARTS):
        pass_on(0, i)

    for copy in w_copies:
        copy.start()

    def send_right(i):
        d1_copy(1, i, True).wait_recv()
        right_copy(i).start()

    @pl.when(x == 2)
    def _():
        send_right(0)

    @pl.when(x == 0)
    def _():
        for i in range(PARTS):
            send_keys(i)

    def bc_copy(by):
        return remote(new.at[which], new.at[which], bc_s.at[by - 1], bc_r.at[which], at_x(by))

    @pl.when(owner)
    def _():
        def arrived(by):
            lag = lax.rem(plane + PLANE - by, PLANE)
            remote(zsum, grad.at[lag], ag_s.at[by - 1], ag_r.at[by - 1], at_plane(by)).wait_recv()

        each(arrived)
        whole = grad[...].reshape(hd, hd)
        norm = jnp.sqrt(jnp.sum(whole * whole)) + 1e-07
        part[0] = whole / norm

        def spread(wide):
            high, low = halves(wide)
            left[:, 0:hd] = high
            left[:, hd : 2 * hd] = low
            left[:, 2 * hd : 3 * hd] = high
            return high, low

        def spread_both(wide):
            high, low = spread(wide)
            right[:, 0:hd] = high
            right[:, hd : 2 * hd] = high
            right[:, 2 * hd : 3 * hd] = low
            return high, low

        def sweep(n, carry):
            high, low = spread_both(part[0])
            stack[0:hd] = high
            stack[hd : 2 * hd] = high
            stack[2 * hd : 3 * hd] = low
            square = dot_nt(left[...], right[...])
            part[1] = square
            spread_both(square)
            part[1] = ns_second * part[1] + ns_third * dot_nt(left[...], right[...])
            spread(part[1])
            part[0] = ns_first * part[0] + dot_nn(left[...], stack[...])

            @pl.when(x == 2)
            def _():
                send_right(n + 1)

            return carry

        lax.fori_loop(0, 5, sweep, 0)
        for m, old in enumerate((gate_w, up_w, down_w)):

            @pl.when(x == m)
            def _(m=m, old=old):
                new[m] = (old[0].astype(F32) - part[0]).astype(BF16)

        for by in (1, 2, 3):
            bc_copy(by).start()

    @pl.when(seq >= 4)
    def _():
        attend(kh.at[3], vh.at[3], 4)

    @pl.when(x != 2)
    def _():
        for i in range(PARTS):
            d1_copy(1, i, True).wait_recv()

    @pl.when(seq >= 1)
    def _():
        attend(kh.at[0], vh.at[0], 1)

    for i in range(PARTS):
        d3_copy(0, i, True).wait_recv()

    @pl.when(seq >= 3)
    def _():
        attend(kh.at[2], vh.at[2], 3)

    for kind in (0, 1):
        for i in range(PARTS):
            d2_copy(kind, i).wait_recv()

    @pl.when(seq >= 2)
    def _():
        attend(kh.at[1], vh.at[1], 2)

    for m in range(3):

        @pl.when(x != m)
        def _():
            remote(new.at[m], new.at[m], bc_s.at[0], bc_r.at[m], at_x(1)).wait_recv()

    def hy_copy(i):
        return remote(comb.at[head, rows(i)], comb.at[head, rows(i)], hy_s.at[i], hy_r.at[i], chip)

    def hc_copy(i):
        return remote(comb.at[head, rows(i)], comb.at[head, rows(i)], hc_s.at[i], hc_r.at[i], core)

    far = (1 - yl) * 2 + c

    def hf_copy(i):
        return remote(comb.at[far, rows(i)], comb.at[far, rows(i)], hf_s.at[i], hf_r.at[i], core)

    for i in range(tiles):
        at = rows(i)
        q_t = q[at, :]
        gate_q = dot_nn(q_t, new[0])
        up_q = dot_nn(q_t, new[1])
        q_hidden = (gate_q * (1.0 / (1.0 + jnp.exp(-gate_q))) * up_q).astype(BF16)
        fast = dot_nn(q_hidden, new[2])
        mean = jnp.mean(fast * fast, axis=1, keepdims=True)
        ttt = fast * lax.rsqrt(mean + 1e-06) * gain[...]
        attended = acc[at, :] / total[at, :][:, :1]
        comb[head, at, :] = (attended + ttt).astype(BF16)
        hy_copy(i).start()
        hc_copy(i).start()

    for i in range(tiles):
        hy_copy(i).wait_recv()
        hf_copy(i).start()

    for copy in w_copies:
        copy.wait()
    wcol[head] = out_w[:, pl.ds(pl.multiple_of(head * hd, 128), hd)]

    for i in range(tiles):
        hc_copy(i).wait_recv()
        hf_copy(i).wait_recv()
        at = rows(i)
        mixed = dot_nn(comb[0, at, :], wcol[0])
        for h in range(1, 4):
            mixed += dot_nn(comb[h, at, :], wcol[h])
        out[at, :] = mixed.astype(BF16)

    for kind in (0, 1):
        for i in range(PARTS):
            row_copy(kind, i).wait_send()
            d1_copy(kind, i, True).wait_send()
            d3_copy(kind, i, True).wait_send()
    for i in range(PARTS):
        d2_copy(0, i).wait_send()

        @pl.when(x > 0)
        def _():
            d2_copy(1, i).wait_send()

        @pl.when(x == 2)
        def _():
            right_copy(i).wait_send()
    for by in (1, 2, 3):
        m, copy = xs_copy(by)

        @pl.when(m < 3)
        def _(copy=copy):
            copy.wait_send()

    @pl.when(owner)
    def _():
        each(lambda by: zs_copy(by).wait_send())
        each(lambda by: ag_copy(by).wait_send())
        for by in (1, 2, 3):
            bc_copy(by).wait_send()

    for i in range(tiles):
        hy_copy(i).wait_send()
        hc_copy(i).wait_send()
        hf_copy(i).wait_send()


def shards(queries, keys, values, learn_rate, gate_fast, up_fast, down_fast, ttt_gain, out_weight):
    tok, hd = queries.shape
    tiles = tok // 256
    piece = hd // PLANE
    dma = lambda n: pltpu.SemaphoreType.DMA((n,))
    scratch = [
        pltpu.VMEM((4, tok, hd), BF16),
        pltpu.VMEM((4, tok, hd), BF16),
        pltpu.VMEM((tok, hd), F32),
        pltpu.VMEM((tok, 128), F32),
        pltpu.VMEM((tok, 128), F32),
        pltpu.VMEM((tok, hd), BF16),
        pltpu.VMEM((tok, hd), BF16),
        pltpu.VMEM((tok, hd), BF16),
        pltpu.VMEM((tok, hd), BF16),
        pltpu.VMEM((3, hd, hd), F32),
        pltpu.VMEM((3, hd, hd), BF16),
        pltpu.VMEM((3, hd, hd), BF16),
        pltpu.VMEM((PLANE, piece, hd), BF16),
        pltpu.VMEM((PLANE - 1, piece, hd), BF16),
        pltpu.VMEM((piece, hd), F32),
        pltpu.VMEM((PLANE, piece, hd), F32),
        pltpu.VMEM((hd, 3 * hd), BF16),
        pltpu.VMEM((hd, 3 * hd), BF16),
        pltpu.VMEM((3 * hd, hd), BF16),
        pltpu.VMEM((3, hd, hd), BF16),
        pltpu.VMEM((4, tok, hd), BF16),
        pltpu.VMEM((4, hd, hd), BF16),
    ]
    scratch += [dma(2 * PARTS)] * 8 + [dma(PARTS)]
    scratch += [dma(3)] * 2 + [dma(PLANE - 1)] * 4 + [dma(3)] * 2
    scratch += [dma(3)] * 2 + [dma(tiles)] * 6
    vmem = pl.BlockSpec(memory_space=pltpu.VMEM)
    return pl.pallas_call(
        layer,
        out_shape=jax.ShapeDtypeStruct((tok, hd), BF16),
        in_specs=[vmem] * 9,
        out_specs=vmem,
        scratch_shapes=scratch,
        compiler_params=pltpu.CompilerParams(
            collective_id=0, has_side_effects=True, vmem_limit_bytes=56 * 1024 * 1024
        ),
        name="layer",
    )(queries, keys, values, learn_rate, gate_fast, up_fast, down_fast, ttt_gain, out_weight)


def solution(mesh):
    torus = Mesh(mesh.devices.reshape(SIZES), AXES)
    in_specs = (
        P(SEQ, HEAD),
        P(SEQ, HEAD),
        P(SEQ, HEAD),
        P(HEAD, SEQ),
        P(HEAD, None, None),
        P(HEAD, None, None),
        P(HEAD, None, None),
        P(HEAD, None),
        P(HEAD, None),
    )
    return jax.shard_map(
        shards, mesh=torus, in_specs=in_specs, out_specs=P(SEQ, HEAD), check_vma=False
    )
```
